32 devices in a mesh: seq: 8 (over z, y), head: 4 (over x, core).
Axes of the slice: x: 2, y: 2, z: 4, core: 2. Of those that a mesh axis runs over, the one named last changes fastest.
Arguments:
- queries: bfloat16 [8192, 4096], P('seq', 'head'), may hold values from -6 to 6
- keys: bfloat16 [8192, 4096], P('seq', 'head'), may hold values from -6 to 6
- values: bfloat16 [8192, 4096], P('seq', 'head'), may hold values from -6 to 6
- out_grad: bfloat16 [8192, 4096], P('seq', 'head'), may hold values from -6 to 6
- level_table: float32 [4, 256], replicated, may hold values from 0.05 to 0.5
- table_index: int32 [8192], P('seq'), may hold values from 0 to 255
- reach: int32 [8], P('seq'), may hold values from 1 to 3, as said below
Outputs:
- query_grad: bfloat16 [8192, 4096], P('seq', 'head')
- key_grad: bfloat16 [8192, 4096], P('seq', 'head')
- value_grad: bfloat16 [8192, 4096], P('seq', 'head')
- table_grad: float32 [4, 256], replicated
The draws below stay inside these ranges and needn't reach their ends.
Inputs may be any that keep to these rules, and one draw needn't show every extreme that they name: Some group has reach 3 and some has reach 1.
All inputs are finite; a program needn't handle non-finite values.
Results may differ from the reference program's by a relative error of at most 0.0056.
Values sent between devices are 32-bit elements; how exact they have to be, the bound alone decides.
A program may use at most 128 MiB of HBM per device.

```python
import math
import jax
import jax.numpy as jnp
from jax import lax

DH = 128
HEADS = 32
L_DEV = 1024
NTAB = 256
LEVELS = 3
TOKENS = 8192
N_SEQ = 8


def draw_reach(key, part):
    reach = jax.random.randint(key, (N_SEQ,), 1, LEVELS + 1)
    order = jax.random.permutation(jax.random.fold_in(key, 7), N_SEQ)
    reach = reach.at[order[0]].set(LEVELS)
    reach = reach.at[order[1]].set(1)
    return reach.astype(jnp.int32)


def set_ends(values, rng, low, high):
    place = [jax.random.randint(jax.random.fold_in(rng, axis), (), 0, length) for axis, length in enumerate(values.shape)]
    main_axis = values.shape.index(max(values.shape))
    neighbour = place[:main_axis] + [(place[main_axis] + 1) % values.shape[main_axis]] + place[main_axis + 1:]
    return values.at[tuple(place)].set(low).at[tuple(neighbour)].set(high)


def steps_of(stream_key, dims, pieces, smallest, top_value):
    level = 1.0
    for dim, blocks in pieces:
        draws = jax.random.uniform(jax.random.fold_in(jax.random.fold_in(stream_key, 6), dim), (blocks,), jnp.float32, smallest / len(pieces), top_value / len(pieces))
        level = level * jnp.repeat(jnp.exp(draws), dims[dim] // blocks).reshape((-1,) + (1,) * (len(dims) - 1 - dim))
    return level


def centred(stream_key, dims, spread, most, split=(), kind=jnp.bfloat16):
    gain = steps_of(stream_key, dims, split, -0.22, 0.18) if split else 1.0
    drawn = jax.random.normal(stream_key, dims, jnp.float32) * spread * gain
    return jnp.minimum(jnp.maximum(drawn, -most), most).astype(kind)


def setup_inputs(seed: int = 0) -> dict:
    key_list = jax.random.split(jax.random.key(seed), 8)
    return {
        "queries": centred(key_list[0], (TOKENS, HEADS * DH), 1.0, 6.0, ((0, 8), (1, 4))),
        "keys": centred(key_list[1], (TOKENS, HEADS * DH), 1.0, 6.0, ((0, 8), (1, 4))),
        "values": centred(key_list[2], (TOKENS, HEADS * DH), 1.0, 6.0, ((0, 8), (1, 4))),
        "out_grad": centred(key_list[3], (TOKENS, HEADS * DH), 1.0, 6.0, ((0, 8), (1, 4))),
        "level_table": jnp.clip(jnp.exp(jax.random.uniform(key_list[4], (LEVELS + 1, NTAB), jnp.float32, math.log(0.05), math.log(0.5))), 0.05, 0.5),
        "table_index": set_ends(jax.random.randint(key_list[5], (TOKENS,), 0, NTAB), jax.random.fold_in(key_list[5], 1), 0, NTAB - 1).astype(jnp.int32),
        "reach": draw_reach(jax.random.fold_in(key_list[7], 71), 0),
    }


precise = lax.Precision.HIGHEST


def rounded(array):
    return lax.optimization_barrier(array.astype(jnp.bfloat16)).astype(jnp.float32)


def level_between(target, source, levels):
    crossed = jnp.bitwise_xor(target, source)
    height = jnp.zeros_like(crossed)
    for exponent in range(levels):
        height = height + (crossed >= 2 ** exponent).astype(jnp.int32)
    return jnp.where(source < target, height, 0)


def reference(queries, keys, values, out_grad, level_table, table_index, reach):
    scale = 1.0 / DH
    count = L_DEV * N_SEQ
    weights = jnp.take(level_table, table_index, axis=1).T
    group_of = jnp.arange(count, dtype=jnp.int32) // L_DEV
    active = (jnp.arange(1, LEVELS + 1, dtype=jnp.int32)[None, :] <= reach[group_of][:, None]).astype(jnp.float32)
    near_weight = weights[:, 0].reshape(N_SEQ, L_DEV)
    far_weight = (weights[:, 1:] * active).reshape(N_SEQ, L_DEV, LEVELS)
    group_ids = jnp.arange(N_SEQ, dtype=jnp.int32)
    height = level_between(group_ids[:, None], group_ids[None, :], LEVELS)
    pick = (height[:, :, None] == jnp.arange(1, LEVELS + 1, dtype=jnp.int32)[None, None, :]).astype(jnp.float32)
    positions = jnp.arange(L_DEV, dtype=jnp.int32)
    causal = (positions[:, None] >= positions[None, :]).astype(jnp.float32)
    coef = scale * near_weight[:, :, None] * causal[None]

    def head_step(carry, head_index):
        start = head_index * DH

        def cut(array):
            return lax.dynamic_slice_in_dim(array, start, DH, 1).astype(jnp.float32).reshape(N_SEQ, L_DEV, DH)

        query_one, key_one, value_one, grad_one = cut(queries), cut(keys), cut(values), cut(out_grad)
        group_state = jnp.einsum("csd,cse->cde", key_one, value_one, precision=precise)
        level_state = jnp.einsum("csl,sde->clde", pick, group_state, precision=precise)
        state_bf = rounded(level_state)
        reads = jnp.einsum("cte,clde->ctld", grad_one, state_bf, precision=precise)
        weighted = rounded(query_one[:, :, None, :] * far_weight[:, :, :, None])
        grad_part = jnp.einsum("ctld,cte->clde", weighted, grad_one, precision=precise)
        returned = jnp.einsum("csl,clde->sde", pick, grad_part, precision=precise)
        returned_bf = rounded(returned)
        scores = jnp.einsum("ctd,csd->cts", query_one, key_one, precision=precise)
        probs = rounded(scores * coef)
        grad_probs = jnp.einsum("cte,cse->cts", grad_one, value_one, precision=precise)
        grad_scores = rounded(grad_probs * coef)
        query_grad = jnp.einsum("cts,csd->ctd", grad_scores, key_one, precision=precise)
        query_grad = query_grad + scale * jnp.sum(reads * far_weight[:, :, :, None], axis=2)
        key_grad = jnp.einsum("cts,ctd->csd", grad_scores, query_one, precision=precise)
        key_grad = key_grad + scale * jnp.einsum("cse,cde->csd", value_one, returned_bf, precision=precise)
        value_grad = jnp.einsum("cts,cte->cse", probs, grad_one, precision=precise)
        value_grad = value_grad + scale * jnp.einsum("csd,cde->cse", key_one, returned_bf, precision=precise)
        near_lambda = scale * jnp.sum(causal[None] * scores * grad_probs, axis=2)
        far_lambda = scale * jnp.sum(reads * query_one[:, :, None, :], axis=3)
        lambda_part = jnp.concatenate([near_lambda[:, :, None], far_lambda], 2).reshape(count, LEVELS + 1)
        outputs = (query_grad.reshape(count, DH).astype(jnp.bfloat16), key_grad.reshape(count, DH).astype(jnp.bfloat16), value_grad.reshape(count, DH).astype(jnp.bfloat16))
        return carry + lambda_part, outputs

    initial = jnp.zeros((count, LEVELS + 1), jnp.float32)
    total, stacked = lax.scan(head_step, initial, jnp.arange(HEADS, dtype=jnp.int32))
    query_grad, key_grad, value_grad = [jnp.transpose(piece, (1, 0, 2)).reshape(count, HEADS * DH) for piece in stacked]
    lambda_grad = total * jnp.concatenate([jnp.ones((count, 1), jnp.float32), active], 1)
    onehot = (table_index[:, None] == jnp.arange(NTAB, dtype=jnp.int32)[None, :]).astype(jnp.float32)
    table_grad = jnp.dot(lambda_grad.T, onehot, precision=precise) / count
    return query_grad, key_grad, value_grad, table_grad
```

```python
import functools

import jax
import jax.numpy as jnp
from jax import lax
from jax.experimental import pallas as pl
from jax.experimental.pallas import tpu as pltpu
from jax.sharding import PartitionSpec as P

DH = 128
BLOCK = 256
CHUNKS = 4
PIECES = 1

HOP = 2.2
GAP = 1.4
LAG = 0.0
MESH = pl.DeviceIdType.MESH
f32 = jnp.float32
bf16 = jnp.bfloat16
NN = (((1,), (0,)), ((), ()))
NT = (((1,), (1,)), ((), ()))
TN = (((0,), (0,)), ((), ()))


def mul(a, b, dims):
    return lax.dot_general(a, b, dims, preferred_element_type=f32)


def split(x):
    high = x.astype(bf16)
    rest = x - high.astype(f32)
    middle = rest.astype(bf16)
    return [high, middle, (rest - middle.astype(f32)).astype(bf16)]


def kernel(
    span, wide, count, levels, heads, length,
    q_hbm, k_hbm, v_hbm, g_hbm, table_ref, index_ref, reach_ref,
    dq_out, dk_out, dv_out, tab_out,
    qb, kb, vb, gb, dqn, dkn, dvn,
    fs, fr, bs, br, acc, stbf, rbf,
    wrow, wcol, lam_near, lam_far, tab1, tab2, onehot,
    in_sem, fsend, frecv, bsend, brecv, t1send, t1recv, t2send, t2recv,
):
    me = lax.axis_index("seq")
    mine = lax.axis_index("head")
    scale = 1.0 / DH
    per = heads // CHUNKS
    ntab = table_ref.shape[1]
    blocks = length // BLOCK

    def load(which, src, dst, h):
        return pltpu.make_async_copy(src.at[:, pl.ds(h * DH, DH)], dst.at[h], in_sem.at[which, h])

    ins = ((2, g_hbm, gb), (3, q_hbm, qb), (0, v_hbm, vb), (1, k_hbm, kb))
    for h in range(heads):
        for which, src, dst in ins:
            load(which, src, dst, h).start()

    barrier = pltpu.get_barrier_semaphore()
    for off in range(1, span):
        pl.semaphore_signal(barrier, inc=1, device_id={"seq": (me + off) % span}, device_id_type=MESH)
    for off in range(1, wide):
        pl.semaphore_signal(barrier, inc=1, device_id={"head": (mine + off) % wide}, device_id_type=MESH)

    top, low = levels - 1, levels - 2
    step = 2 ** low
    quarter = me // step
    bits = [(me // 2 ** b) % 2 for b in range(levels)]
    odd = bits[low] == 1
    even = bits[low] == 0
    f_sends, f_gets, b_sends, b_gets, f_to, b_to = [], [], [], [], [], []
    for b in range(levels):
        partner = me + (1 - 2 * bits[b]) * 2 ** b
        if b < low:
            clear_above = (me // 2 ** (b + 1)) < (span // 2 ** (b + 1) - 1)
            sends = jnp.logical_or(bits[b] == 0, clear_above)
            gets = jnp.logical_or(bits[b] == 1, clear_above)
            f_sends.append(sends)
            f_gets.append(gets)
            b_sends.append(gets)
            b_gets.append(sends)
            f_to.append(partner)
            b_to.append(partner)
        else:
            inner = jnp.logical_or(quarter == 1, quarter == 2)
            f_sends.append(even if b == low else inner)
            f_gets.append(odd if b == low else quarter >= 2)
            b_sends.append(odd if b == low else quarter >= 2)
            b_gets.append(even if b == low else inner)
            f_to.append((me + step) % span)
            b_to.append((me + span - step) % span)

    def part(c):
        return pl.ds(c * per, per)

    def f_copy(b, c, relay=False):
        src = fr if relay else fs
        return pltpu.make_async_remote_copy(
            src_ref=src.at[b, part(c)], dst_ref=fr.at[b, part(c)], send_sem=fsend.at[b, c], recv_sem=frecv.at[b, c],
            device_id={"seq": f_to[b]}, device_id_type=MESH)

    def b_copy(b, c):
        return pltpu.make_async_remote_copy(
            src_ref=bs.at[b, part(c)], dst_ref=br.at[b, part(c)], send_sem=bsend.at[b, c], recv_sem=brecv.at[b, c],
            device_id={"seq": b_to[b]}, device_id_type=MESH)

    def f_start(b, c):
        @pl.when(f_sends[b])
        def _():
            f_copy(b, c).start()

    def b_start(b, c):
        @pl.when(b_sends[b])
        def _():
            b_copy(b, c).start()

    def f_keep(b, c):
        stbf[part(c), :, pl.ds(b * DH, DH)] = fr[b, part(c)].astype(bf16)

    def f_stage(b, c):
        @pl.when(f_gets[b])
        def _():
            f_copy(b, c).wait_recv()
            fs[b + 1, part(c)] = fs[b, part(c)] + fr[b, part(c)]

        f_start(b + 1, c)

        @pl.when(bits[b] == 1)
        def _():
            f_keep(b, c)

    def f_hop(c):
        @pl.when(odd)
        def _():
            f_copy(low, c).wait_recv()
            f_keep(low, c)

        @pl.when(quarter == 1)
        def _():
            fs[top, part(c)] = fs[low, part(c)] + fr[low, part(c)]
            f_copy(top, c).start()

    def f_relay(c):
        @pl.when(quarter == 2)
        def _():
            f_copy(top, c).wait_recv()
            f_copy(top, c, True).start()
            f_keep(top, c)

    def f_last(c):
        @pl.when(quarter == 3)
        def _():
            f_copy(top, c).wait_recv()
            f_keep(top, c)

    def b_next(b, c):
        bs[b, part(c)] = bs[b, part(c)] + acc[part(c)]
        b_start(b, c)

    def b_relay(c):
        @pl.when(quarter == 2)
        def _():
            b_copy(top, c).wait_recv()
            bs[top, part(c)] = bs[top, part(c)] + br[top, part(c)]
            b_copy(top, c).start()

    def b_turn(c):
        @pl.when(quarter == 1)
        def _():
            b_copy(top, c).wait_recv()
            acc[part(c)] = br[top, part(c)]
            bs[low, part(c)] = bs[low, part(c)] + br[top, part(c)]
            b_copy(low, c).start()
            b_next(low - 1, c)

    def b_hop(c):
        @pl.when(even)
        def _():
            b_copy(low, c).wait_recv()
            acc[part(c)] = br[low, part(c)]
            b_next(low - 1, c)

    def b_stage(b, c):
        @pl.when(b_gets[b])
        def _():
            b_copy(b, c).wait_recv()
            acc[part(c)] = acc[part(c)] + br[b, part(c)]

        if b > 0:
            b_next(b - 1, c)
        else:
            rbf[part(c)] = acc[part(c)].astype(bf16)

    def state_step(h, carry):
        load(0, v_hbm, vb, h).wait()
        load(1, k_hbm, kb, h).wait()
        fs[0, h] = mul(vb[h], kb[h], TN)
        return carry

    def part_step(h, carry):
        load(2, g_hbm, gb, h).wait()
        load(3, q_hbm, qb, h).wait()
        q = qb[h].astype(f32)
        weighted = jnp.concatenate([(q * wcol[l]).astype(bf16) for l in range(levels)], 1)
        whole = mul(gb[h], weighted, TN)
        for l in range(levels):
            bs[l, h] = whole[:, l * DH:(l + 1) * DH] * bits[l].astype(f32)
        return carry

    acc[...] = jnp.zeros(acc.shape, f32)
    stbf[...] = jnp.zeros(stbf.shape, bf16)
    lam_near[...] = jnp.zeros(lam_near.shape, f32)
    lam_far[...] = jnp.zeros(lam_far.shape, f32)
    onehot[...] = (lax.broadcasted_iota(jnp.int32, (ntab, length), 0) == index_ref[...]).astype(f32).astype(bf16)
    rows = sum(mul(x, onehot[...], NN) for x in split(table_ref[...]))
    active = (lax.broadcasted_iota(jnp.int32, (levels + 1, 1), 0) <= reach_ref[0]).astype(f32)
    rows = rows * active
    wrow[...] = rows[0:1] * scale
    lane_level = lax.broadcasted_iota(jnp.int32, (levels + 1, levels * DH), 1) // DH + 1
    pick = (lax.broadcasted_iota(jnp.int32, (levels + 1, levels * DH), 0) == lane_level).astype(f32).astype(bf16)
    spread = mul(jnp.concatenate(split(rows), 0), jnp.concatenate([pick] * 3, 0), TN)
    for l in range(levels):
        wcol[l] = spread[:, l * DH:(l + 1) * DH]

    for c in range(CHUNKS):
        lax.fori_loop(c * per, (c + 1) * per, part_step, 0)
        lax.fori_loop(c * per, (c + 1) * per, state_step, 0)
        if c == 0:
            pl.semaphore_wait(barrier, span - 1 + wide - 1)
        f_start(0, c)

        @pl.when(quarter == 3)
        def _():
            b_copy(top, c).start()
            b_start(low - 1, c)
    for c in range(CHUNKS):
        @pl.when(quarter == 3)
        def _():
            b_copy(low, c).start()

    timed = []
    for c in range(CHUNKS):
        for b in range(low):
            timed.append((HOP * (b + 1) + GAP * c, functools.partial(f_stage, b), c))
        base = HOP * low + GAP * c
        timed.append((base + HOP, f_hop, c))
        timed.append((base + 2 * HOP, f_relay, c))
        timed.append((base + 3 * HOP, f_last, c))
        base = LAG + GAP * c
        timed.append((base + HOP, b_relay, c))
        timed.append((base + 2 * HOP, b_turn, c))
        timed.append((base + 3 * HOP, b_hop, c))
    timed.sort(key=lambda item: item[0])
    inside = [(max(0, int(when)), run, c) for when, run, c in timed if when < heads]
    after = [(run, c) for when, run, c in timed if when >= heads]

    def near_step(h, carry):
        for slot in sorted({item[0] for item in inside}):
            @pl.when(h == slot)
            def _():
                for when, run, c in inside:
                    if when == slot:
                        run(c)

        causal = lax.broadcasted_iota(jnp.int32, (BLOCK, BLOCK), 1) >= lax.broadcasted_iota(jnp.int32, (BLOCK, BLOCK), 0)
        for j in range(blocks):
            start, stop = j * BLOCK, (j + 1) * BLOCK
            rest = length - start
            k_j = kb[h, start:stop]
            v_j = vb[h, start:stop]
            q_r = qb[h, start:]
            g_r = gb[h, start:]
            scores = mul(k_j, q_r, NT)
            grads = mul(v_j, g_r, NT)
            s_parts, g_parts = [], []
            for i in range(rest // BLOCK):
                s_i = scores[:, i * BLOCK:(i + 1) * BLOCK]
                g_i = grads[:, i * BLOCK:(i + 1) * BLOCK]
                if i == 0:
                    s_i = jnp.where(causal, s_i, 0.0)
                    g_i = jnp.where(causal, g_i, 0.0)
                at = slice(start + i * BLOCK, start + (i + 1) * BLOCK)
                w_i = wrow[:, at]
                lam_near[:, at] += jnp.sum((s_i * g_i).reshape(BLOCK // 8, 8, BLOCK), axis=0)
                s_parts.append((s_i * w_i).astype(bf16))
                g_parts.append((g_i * w_i).astype(bf16))
            probs = jnp.concatenate(s_parts, 1)
            gsc = jnp.concatenate(g_parts, 1)
            dvn[h, start:stop] = mul(probs, g_r, NN)
            dkn[h, start:stop] = mul(gsc, q_r, NN)
            dq = mul(gsc, k_j, TN)
            if j == 0:
                dqn[h] = dq
            else:
                dqn[h, start:] += dq
        return carry

    lax.fori_loop(0, heads, near_step, 0)
    near_row = jnp.sum(lam_near[...], axis=0, keepdims=True)
    near_sum = mul(jnp.concatenate(split(near_row), 0), onehot[...], NT)
    tab1[me, 0:1] = jnp.sum(near_sum, axis=0, keepdims=True)

    def query_step(h, carry):
        cols = pl.ds(pl.multiple_of(h * DH, DH), DH)
        for i in range(blocks):
            at = slice(i * BLOCK, (i + 1) * BLOCK)
            reads = mul(gb[h, at], stbf[h], NN)
            q = qb[h, at].astype(f32)
            far = None
            for l in range(levels):
                read = reads[:, l * DH:(l + 1) * DH]
                lam_far[l, at] += q * read
                term = read * wcol[l, at]
                far = term if far is None else far + term
            dq_out[at, cols] = (dqn[h, at] + scale * far).astype(bf16)
        return carry

    def key_step(h, carry):
        cols = pl.ds(pl.multiple_of(h * DH, DH), DH)
        for i in range(blocks):
            at = slice(i * BLOCK, (i + 1) * BLOCK)
            dk_out[at, cols] = (dkn[h, at] + scale * mul(vb[h, at], rbf[h], NN)).astype(bf16)
            dv_out[at, cols] = (dvn[h, at] + scale * mul(kb[h, at], rbf[h], NT)).astype(bf16)
        return carry

    for c in range(CHUNKS):
        while any(run is f_last and late <= c for run, late in after):
            run, late = after.pop(0)
            run(late)
        lax.fori_loop(c * per, (c + 1) * per, query_step, 0)
    for run, late in after:
        run(late)

    lane = lax.broadcasted_iota(jnp.int32, (length, DH), 1)
    columns = jnp.zeros((length, DH), f32)
    for l in range(levels):
        columns = jnp.where(lane % levels == l, jnp.sum(lam_far[l], axis=1, keepdims=True), columns)
    thirds = split(columns)
    third = jnp.where(lane < levels, thirds[0].astype(f32), jnp.where(lane < 2 * levels, thirds[1].astype(f32), thirds[2].astype(f32)))
    turned = mul(onehot[...], third.astype(bf16), NN).T
    far_sum = turned[0:levels] + turned[levels:2 * levels] + turned[2 * levels:3 * levels]
    tab1[me] = jnp.concatenate([tab1[me, 0:1], far_sum], 0) * active * (scale / count)

    def t1_copy(off):
        return pltpu.make_async_remote_copy(
            src_ref=tab1.at[me], dst_ref=tab1.at[me], send_sem=t1send.at[off], recv_sem=t1recv.at[off],
            device_id={"seq": (me + off) % span}, device_id_type=MESH)

    def t1_from(off):
        place = (me + span - off) % span
        return pltpu.make_async_remote_copy(
            src_ref=tab1.at[place], dst_ref=tab1.at[place], send_sem=t1send.at[off], recv_sem=t1recv.at[off],
            device_id={"seq": (me + off) % span}, device_id_type=MESH)

    def t2_copy(off):
        return pltpu.make_async_remote_copy(
            src_ref=tab2.at[mine], dst_ref=tab2.at[mine], send_sem=t2send.at[off], recv_sem=t2recv.at[off],
            device_id={"head": (mine + off) % wide}, device_id_type=MESH)

    def t2_from(off):
        place = (mine + wide - off) % wide
        return pltpu.make_async_remote_copy(
            src_ref=tab2.at[place], dst_ref=tab2.at[place], send_sem=t2send.at[off], recv_sem=t2recv.at[off],
            device_id={"head": (mine + off) % wide}, device_id_type=MESH)

    for c in range(CHUNKS):
        for b in range(low - 1, -1, -1):
            b_stage(b, c)
        if c == 0:
            for off in range(1, span):
                t1_copy(off).start()
        lax.fori_loop(c * per, (c + 1) * per, key_step, 0)
        if c == CHUNKS - 2:
            for off in range(1, span):
                t1_from(off).wait_recv()
            total = tab1[0]
            for s in range(1, span):
                total = total + tab1[s]
            tab2[mine] = total
        if c == CHUNKS - 1:
            for off in range(1, wide):
                t2_from(off).wait_recv()
            total = tab2[0]
            for s in range(1, wide):
                total = total + tab2[s]
            tab_out[...] = total
        elif c == CHUNKS - 2:
            for off in range(1, wide):
                t2_copy(off).start()

    for off in range(1, span):
        t1_copy(off).wait_send()
    for off in range(1, wide):
        t2_copy(off).wait_send()
    for b in range(levels):
        for c in range(CHUNKS):
            @pl.when(f_sends[b])
            def _():
                f_copy(b, c).wait_send()

            @pl.when(b_sends[b])
            def _():
                b_copy(b, c).wait_send()


def finish(*refs):
    sem = refs[-1]
    half = (len(refs) - 1) // 2
    copies = []
    for src, dst in zip(refs[:half], refs[half:-1]):
        pieces = PIECES if src.shape[0] > DH else 1
        rows = src.shape[0] // pieces
        for piece in range(pieces):
            at = pl.ds(piece * rows, rows)
            copies.append(pltpu.make_async_copy(src.at[at], dst.at[at], sem.at[len(copies)]))
    for copy in copies:
        copy.start()
    for copy in copies:
        copy.wait()


def local(queries, keys, values, out_grad, level_table, table_index, reach):
    length = queries.shape[0]
    heads = queries.shape[1] // DH
    levels = level_table.shape[0] - 1
    span = lax.axis_size("seq")
    wide = lax.axis_size("head")
    any_spec = pl.BlockSpec(memory_space=pl.ANY)
    vmem = pl.BlockSpec(memory_space=pltpu.VMEM)
    dma = pltpu.SemaphoreType.DMA
    big = jax.ShapeDtypeStruct(queries.shape, bf16)
    outs = (big, big, big, jax.ShapeDtypeStruct(level_table.shape, f32))
    hbm = pl.BlockSpec(memory_space=pltpu.HBM)
    body = functools.partial(kernel, span, wide, length * span, levels, heads, length)
    strip = (heads, length, DH)
    square = (levels, heads, DH, DH)
    parts = pl.pallas_call(
        body,
        out_shape=outs,
        in_specs=[any_spec] * 4 + [vmem, vmem, pl.BlockSpec(memory_space=pltpu.SMEM)],
        out_specs=(vmem, vmem, vmem, vmem),
        scratch_shapes=[
            pltpu.VMEM(strip, bf16), pltpu.VMEM(strip, bf16), pltpu.VMEM(strip, bf16), pltpu.VMEM(strip, bf16),
            pltpu.VMEM(strip, f32), pltpu.VMEM(strip, f32), pltpu.VMEM(strip, f32),
            pltpu.VMEM(square, f32), pltpu.VMEM(square, f32), pltpu.VMEM(square, f32), pltpu.VMEM(square, f32),
            pltpu.VMEM((heads, DH, DH), f32),
            pltpu.VMEM((heads, DH, levels * DH), bf16),
            pltpu.VMEM((heads, DH, DH), bf16),
            pltpu.VMEM((1, length), f32),
            pltpu.VMEM((levels, length, DH), f32),
            pltpu.VMEM((8, length), f32),
            pltpu.VMEM((levels, length, DH), f32),
            pltpu.VMEM((span,) + level_table.shape, f32),
            pltpu.VMEM((wide,) + level_table.shape, f32),
            pltpu.VMEM((level_table.shape[1], length), bf16),
            dma((4, heads)),
            dma((levels, CHUNKS)), dma((levels, CHUNKS)), dma((levels, CHUNKS)), dma((levels, CHUNKS)),
            dma((span,)), dma((span,)), dma((wide,)), dma((wide,)),
        ],
        compiler_params=pltpu.CompilerParams(
            collective_id=0, has_side_effects=True, vmem_limit_bytes=46 * 2 ** 20
        ),
        name="loglinear",
    )(queries, keys, values, out_grad, level_table, table_index.reshape(1, length), reach)
    return pl.pallas_call(
        finish,
        out_shape=outs,
        in_specs=[vmem] * 4,
        out_specs=(hbm, hbm, hbm, hbm),
        scratch_shapes=[dma((3 * PIECES + 1,))],
        compiler_params=pltpu.CompilerParams(vmem_limit_bytes=2 ** 20),
        name="finish",
    )(*parts)


def solution(mesh):
    return jax.shard_map(
        local,
        mesh=mesh,
        in_specs=(
            P("seq", "head"),
            P("seq", "head"),
            P("seq", "head"),
            P("seq", "head"),
            P(),
            P("seq"),
            P("seq"),
        ),
        out_specs=(P("seq", "head"), P("seq", "head"), P("seq", "head"), P()),
        check_vma=False,
    )
```

```python
import functools

import jax
import jax.numpy as jnp
from jax import lax
from jax.experimental import pallas as pl
from jax.experimental.pallas import tpu as pltpu
from jax.sharding import PartitionSpec as P

DH = 128
BLOCK = 256
CHUNKS = 4
PIECES = 1

HOP = 2.2
GAP = 1.4
LAG = 0.0
LEAD = 1.0
MESH = pl.DeviceIdType.MESH
f32 = jnp.float32
bf16 = jnp.bfloat16
NN = (((1,), (0,)), ((), ()))
NT = (((1,), (1,)), ((), ()))
TN = (((0,), (0,)), ((), ()))


def mul(a, b, dims):
    return lax.dot_general(a, b, dims, preferred_element_type=f32)


def split(x):
    high = x.astype(bf16)
    rest = x - high.astype(f32)
    middle = rest.astype(bf16)
    return [high, middle, (rest - middle.astype(f32)).astype(bf16)]


def kernel(
    span, wide, count, levels, heads, length,
    q_hbm, k_hbm, v_hbm, g_hbm, table_ref, index_ref, reach_ref,
    dq_out, dk_out, dv_out, tab_out,
    qb, kb, vb, gb, dqn, dkn, dvn,
    fs, fr, bs, br, acc, stbf, rbf,
    wrow, wcol, lam_near, lam_far, tab1, tab2, onehot,
    in_sem, know, fsend, frecv, bsend, brecv, t1send, t1recv, t2send, t2recv,
):
    me = lax.axis_index("seq")
    mine = lax.axis_index("head")
    scale = 1.0 / DH
    per = heads // CHUNKS
    ntab = table_ref.shape[1]
    blocks = length // BLOCK

    def load(which, src, dst, h):
        return pltpu.make_async_copy(src.at[:, pl.ds(h * DH, DH)], dst.at[h], in_sem.at[which, h])

    ins = ((2, g_hbm, gb), (3, q_hbm, qb), (0, v_hbm, vb), (1, k_hbm, kb))
    for h in range(heads):
        for which, src, dst in ins:
            load(which, src, dst, h).start()

    top, low = levels - 1, levels - 2
    step = 2 ** low
    quarter = me // step
    bits = [(me // 2 ** b) % 2 for b in range(levels)]
    odd = bits[low] == 1
    even = bits[low] == 0
    inner = jnp.logical_or(quarter == 1, quarter == 2)
    up, down = (me + step) % span, (me + span - step) % span
    partners = [me + (1 - 2 * bits[b]) * 2 ** b for b in range(low)]

    def greet(sem):
        for partner in partners:
            pl.semaphore_signal(sem, inc=1, device_id={"seq": partner}, device_id_type=MESH)

        @pl.when(quarter < 3)
        def _():
            pl.semaphore_signal(sem, inc=1, device_id={"seq": up}, device_id_type=MESH)

        @pl.when(quarter > 0)
        def _():
            pl.semaphore_signal(sem, inc=1, device_id={"seq": down}, device_id_type=MESH)

    near_by = low + 1 + inner.astype(jnp.int32)
    barrier = pltpu.get_barrier_semaphore()
    greet(barrier)
    for off in range(1, wide):
        pl.semaphore_signal(barrier, inc=1, device_id={"head": (mine + off) % wide}, device_id_type=MESH)

    def hear(r):
        pl.semaphore_wait(know.at[r], near_by)
        if r + 1 < low + 2:
            greet(know.at[r + 1])

    f_sends, f_gets, b_sends, b_gets, f_to, b_to = [], [], [], [], [], []
    for b in range(levels):
        partner = me + (1 - 2 * bits[b]) * 2 ** b
        if b < low:
            clear_above = (me // 2 ** (b + 1)) < (span // 2 ** (b + 1) - 1)
            sends = jnp.logical_or(bits[b] == 0, clear_above)
            gets = jnp.logical_or(bits[b] == 1, clear_above)
            f_sends.append(sends)
            f_gets.append(gets)
            b_sends.append(gets)
            b_gets.append(sends)
            f_to.append(partner)
            b_to.append(partner)
        else:
            inner = jnp.logical_or(quarter == 1, quarter == 2)
            f_sends.append(even if b == low else inner)
            f_gets.append(odd if b == low else quarter >= 2)
            b_sends.append(odd if b == low else quarter >= 2)
            b_gets.append(even if b == low else inner)
            f_to.append((me + step) % span)
            b_to.append((me + span - step) % span)

    def part(c):
        return pl.ds(c * per, per)

    def f_copy(b, c, relay=False):
        src = fr if relay else fs
        return pltpu.make_async_remote_copy(
            src_ref=src.at[b, part(c)], dst_ref=fr.at[b, part(c)], send_sem=fsend.at[b, c], recv_sem=frecv.at[b, c],
            device_id={"seq": f_to[b]}, device_id_type=MESH)

    def b_copy(b, c):
        return pltpu.make_async_remote_copy(
            src_ref=bs.at[b, part(c)], dst_ref=br.at[b, part(c)], send_sem=bsend.at[b, c], recv_sem=brecv.at[b, c],
            device_id={"seq": b_to[b]}, device_id_type=MESH)

    def f_start(b, c):
        @pl.when(f_sends[b])
        def _():
            f_copy(b, c).start()

    def b_start(b, c):
        @pl.when(b_sends[b])
        def _():
            b_copy(b, c).start()

    def f_keep(b, c):
        stbf[part(c), :, pl.ds(b * DH, DH)] = fr[b, part(c)].astype(bf16)

    def f_stage(b, c):
        @pl.when(f_gets[b])
        def _():
            f_copy(b, c).wait_recv()
            fs[b + 1, part(c)] = fs[b, part(c)] + fr[b, part(c)]

        f_start(b + 1, c)

        @pl.when(bits[b] == 1)
        def _():
            f_keep(b, c)

    def f_hop(c):
        @pl.when(odd)
        def _():
            f_copy(low, c).wait_recv()
            f_keep(low, c)

        @pl.when(quarter == 1)
        def _():
            fs[top, part(c)] = fs[low, part(c)] + fr[low, part(c)]
            f_copy(top, c).start()

    def f_relay(c):
        @pl.when(quarter == 2)
        def _():
            f_copy(top, c).wait_recv()
            f_copy(top, c, True).start()
            f_keep(top, c)

    def f_last(c):
        @pl.when(quarter == 3)
        def _():
            f_copy(top, c).wait_recv()
            f_keep(top, c)

    def b_next(b, c):
        bs[b, part(c)] = bs[b, part(c)] + acc[part(c)]
        b_start(b, c)

    def b_relay(c):
        @pl.when(quarter == 2)
        def _():
            b_copy(top, c).wait_recv()
            bs[top, part(c)] = bs[top, part(c)] + br[top, part(c)]
            b_copy(top, c).start()

    def b_turn(c):
        @pl.when(quarter == 1)
        def _():
            b_copy(top, c).wait_recv()
            acc[part(c)] = br[top, part(c)]
            bs[low, part(c)] = bs[low, part(c)] + br[top, part(c)]
            b_copy(low, c).start()
            b_next(low - 1, c)

    def b_hop(c):
        @pl.when(even)
        def _():
            b_copy(low, c).wait_recv()
            acc[part(c)] = br[low, part(c)]
            b_next(low - 1, c)

    def b_stage(b, c):
        @pl.when(b_gets[b])
        def _():
            b_copy(b, c).wait_recv()
            acc[part(c)] = acc[part(c)] + br[b, part(c)]

        if b > 0:
            b_next(b - 1, c)
        else:
            rbf[part(c)] = acc[part(c)].astype(bf16)

    def state_step(h, carry):
        load(0, v_hbm, vb, h).wait()
        load(1, k_hbm, kb, h).wait()
        fs[0, h] = mul(vb[h], kb[h], TN)
        return carry

    def part_step(h, carry):
        load(2, g_hbm, gb, h).wait()
        load(3, q_hbm, qb, h).wait()
        q = qb[h].astype(f32)
        weighted = jnp.concatenate([(q * wcol[l]).astype(bf16) for l in range(levels)], 1)
        whole = mul(gb[h], weighted, TN)
        for l in range(levels):
            bs[l, h] = whole[:, l * DH:(l + 1) * DH] * bits[l].astype(f32)
        return carry

    acc[...] = jnp.zeros(acc.shape, f32)
    stbf[...] = jnp.zeros(stbf.shape, bf16)
    lam_near[...] = jnp.zeros(lam_near.shape, f32)
    lam_far[...] = jnp.zeros(lam_far.shape, f32)
    onehot[...] = (lax.broadcasted_iota(jnp.int32, (ntab, length), 0) == index_ref[...]).astype(f32).astype(bf16)
    rows = sum(mul(x, onehot[...], NN) for x in split(table_ref[...]))
    active = (lax.broadcasted_iota(jnp.int32, (levels + 1, 1), 0) <= reach_ref[0]).astype(f32)
    rows = rows * active
    wrow[...] = rows[0:1] * scale
    lane_level = lax.broadcasted_iota(jnp.int32, (levels + 1, levels * DH), 1) // DH + 1
    pick = (lax.broadcasted_iota(jnp.int32, (levels + 1, levels * DH), 0) == lane_level).astype(f32).astype(bf16)
    spread = mul(jnp.concatenate(split(rows), 0), jnp.concatenate([pick] * 3, 0), TN)
    for l in range(levels):
        wcol[l] = spread[:, l * DH:(l + 1) * DH]

    for c in range(CHUNKS):
        lax.fori_loop(c * per, (c + 1) * per, part_step, 0)
        lax.fori_loop(c * per, (c + 1) * per, state_step, 0)
        if c == 0:
            pl.semaphore_wait(barrier, near_by + wide - 1)
            greet(know.at[0])
        f_start(0, c)

        @pl.when(quarter == 3)
        def _():
            b_copy(top, c).start()
            b_start(low - 1, c)
    for c in range(CHUNKS):
        @pl.when(quarter == 3)
        def _():
            b_copy(low, c).start()

    timed = []
    for c in range(CHUNKS):
        for b in range(low):
            timed.append((HOP * (b + 1) + GAP * c - LEAD, functools.partial(f_stage, b), c))
        base = HOP * low + GAP * c - LEAD
        timed.append((min(base + HOP, heads + 0.4 + 0.01 * c), f_hop, c))
        timed.append((min(base + 2 * HOP, heads + 0.5 + 0.01 * c), f_relay, c))
        timed.append((base + 3 * HOP, f_last, c))
        base = LAG + GAP * c
        timed.append((base + HOP, b_relay, c))
        timed.append((base + 2 * HOP, b_turn, c))
        timed.append((base + 3 * HOP, b_hop, c))
    for r in range(low + 2):
        timed.append((2.0 + r, lambda c, r=r: hear(r), 0))
    timed.sort(key=lambda item: item[0])
    inside = [(max(0, int(when)), run, c) for when, run, c in timed if when < heads]
    after = [(run, c) for when, run, c in timed if when >= heads]

    def near_step(h, carry):
        for slot in sorted({item[0] for item in inside}):
            @pl.when(h == slot)
            def _():
                for when, run, c in inside:
                    if when == slot:
                        run(c)

        causal = lax.broadcasted_iota(jnp.int32, (BLOCK, BLOCK), 1) >= lax.broadcasted_iota(jnp.int32, (BLOCK, BLOCK), 0)
        for j in range(blocks):
            start, stop = j * BLOCK, (j + 1) * BLOCK
            rest = length - start
            k_j = kb[h, start:stop]
            v_j = vb[h, start:stop]
            q_r = qb[h, start:]
            g_r = gb[h, start:]
            scores = mul(k_j, q_r, NT)
            grads = mul(v_j, g_r, NT)
            s_parts, g_parts = [], []
            for i in range(rest // BLOCK):
                s_i = scores[:, i * BLOCK:(i + 1) * BLOCK]
                g_i = grads[:, i * BLOCK:(i + 1) * BLOCK]
                if i == 0:
                    s_i = jnp.where(causal, s_i, 0.0)
                    g_i = jnp.where(causal, g_i, 0.0)
                at = slice(start + i * BLOCK, start + (i + 1) * BLOCK)
                w_i = wrow[:, at]
                lam_near[:, at] += jnp.sum((s_i * g_i).reshape(BLOCK // 8, 8, BLOCK), axis=0)
                s_parts.append((s_i * w_i).astype(bf16))
                g_parts.append((g_i * w_i).astype(bf16))
            probs = jnp.concatenate(s_parts, 1)
            gsc = jnp.concatenate(g_parts, 1)
            dvn[h, start:stop] = mul(probs, g_r, NN)
            dkn[h, start:stop] = mul(gsc, q_r, NN)
            dq = mul(gsc, k_j, TN)
            if j == 0:
                dqn[h] = dq
            else:
                dqn[h, start:] += dq
        return carry

    lax.fori_loop(0, heads, near_step, 0)
    near_row = jnp.sum(lam_near[...], axis=0, keepdims=True)
    near_sum = mul(jnp.concatenate(split(near_row), 0), onehot[...], NT)
    tab1[me, 0:1] = jnp.sum(near_sum, axis=0, keepdims=True)

    def query_step(h, carry):
        cols = pl.ds(pl.multiple_of(h * DH, DH), DH)
        for i in range(blocks):
            at = slice(i * BLOCK, (i + 1) * BLOCK)
            reads = mul(gb[h, at], stbf[h], NN)
            q = qb[h, at].astype(f32)
            far = None
            for l in range(levels):
                read = reads[:, l * DH:(l + 1) * DH]
                lam_far[l, at] += q * read
                term = read * wcol[l, at]
                far = term if far is None else far + term
            dq_out[at, cols] = (dqn[h, at] + scale * far).astype(bf16)
        return carry

    def key_step(h, carry):
        cols = pl.ds(pl.multiple_of(h * DH, DH), DH)
        for i in range(blocks):
            at = slice(i * BLOCK, (i + 1) * BLOCK)
            dk_out[at, cols] = (dkn[h, at] + scale * mul(vb[h, at], rbf[h], NN)).astype(bf16)
            dv_out[at, cols] = (dvn[h, at] + scale * mul(kb[h, at], rbf[h], NT)).astype(bf16)
        return carry

    for c in range(CHUNKS):
        while any(run is f_last and late <= c for run, late in after):
            run, late = after.pop(0)
            run(late)
        lax.fori_loop(c * per, (c + 1) * per, query_step, 0)
    for run, late in after:
        if run is not b_hop:
            run(late)

    lane = lax.broadcasted_iota(jnp.int32, (length, DH), 1)
    columns = jnp.zeros((length, DH), f32)
    for l in range(levels):
        columns = jnp.where(lane % levels == l, jnp.sum(lam_far[l], axis=1, keepdims=True), columns)
    thirds = split(columns)
    third = jnp.where(lane < levels, thirds[0].astype(f32), jnp.where(lane < 2 * levels, thirds[1].astype(f32), thirds[2].astype(f32)))
    turned = mul(onehot[...], third.astype(bf16), NN).T
    far_sum = turned[0:levels] + turned[levels:2 * levels] + turned[2 * levels:3 * levels]
    tab1[me] = jnp.concatenate([tab1[me, 0:1], far_sum], 0) * active * (scale / count)

    def t1_copy(off):
        return pltpu.make_async_remote_copy(
            src_ref=tab1.at[me], dst_ref=tab1.at[me], send_sem=t1send.at[off], recv_sem=t1recv.at[off],
            device_id={"seq": (me + off) % span}, device_id_type=MESH)

    def t1_from(off):
        place = (me + span - off) % span
        return pltpu.make_async_remote_copy(
            src_ref=tab1.at[place], dst_ref=tab1.at[place], send_sem=t1send.at[off], recv_sem=t1recv.at[off],
            device_id={"seq": (me + off) % span}, device_id_type=MESH)

    def t2_copy(off):
        return pltpu.make_async_remote_copy(
            src_ref=tab2.at[mine], dst_ref=tab2.at[mine], send_sem=t2send.at[off], recv_sem=t2recv.at[off],
            device_id={"head": (mine + off) % wide}, device_id_type=MESH)

    def t2_from(off):
        place = (mine + wide - off) % wide
        return pltpu.make_async_remote_copy(
            src_ref=tab2.at[place], dst_ref=tab2.at[place], send_sem=t2send.at[off], recv_sem=t2recv.at[off],
            device_id={"head": (mine + off) % wide}, device_id_type=MESH)

    for off in range(1, span):
        t1_copy(off).start()
    for run, late in after:
        if run is b_hop:
            run(late)
    for c in range(CHUNKS):
        for b in range(low - 1, -1, -1):
            b_stage(b, c)
        lax.fori_loop(c * per, (c + 1) * per, key_step, 0)
        if c == CHUNKS - 2:
            for off in range(1, span):
                t1_from(off).wait_recv()
            total = tab1[0]
            for s in range(1, span):
                total = total + tab1[s]
            tab2[mine] = total
        if c == CHUNKS - 1:
            for off in range(1, wide):
                t2_from(off).wait_recv()
            total = tab2[0]
            for s in range(1, wide):
                total = total + tab2[s]
            tab_out[...] = total
        elif c == CHUNKS - 2:
            for off in range(1, wide):
                t2_copy(off).start()

    for off in range(1, span):
        t1_copy(off).wait_send()
    for off in range(1, wide):
        t2_copy(off).wait_send()
    for b in range(levels):
        for c in range(CHUNKS):
            @pl.when(f_sends[b])
            def _():
                f_copy(b, c).wait_send()

            @pl.when(b_sends[b])
            def _():
                b_copy(b, c).wait_send()


def finish(*refs):
    sem = refs[-1]
    half = (len(refs) - 1) // 2
    copies = []
    for src, dst in zip(refs[:half], refs[half:-1]):
        pieces = PIECES if src.shape[0] > DH else 1
        rows = src.shape[0] // pieces
        for piece in range(pieces):
            at = pl.ds(piece * rows, rows)
            copies.append(pltpu.make_async_copy(src.at[at], dst.at[at], sem.at[len(copies)]))
    for copy in copies:
        copy.start()
    for copy in copies:
        copy.wait()


def local(queries, keys, values, out_grad, level_table, table_index, reach):
    length = queries.shape[0]
    heads = queries.shape[1] // DH
    levels = level_table.shape[0] - 1
    span = lax.axis_size("seq")
    wide = lax.axis_size("head")
    any_spec = pl.BlockSpec(memory_space=pl.ANY)
    vmem = pl.BlockSpec(memory_space=pltpu.VMEM)
    dma = pltpu.SemaphoreType.DMA
    big = jax.ShapeDtypeStruct(queries.shape, bf16)
    outs = (big, big, big, jax.ShapeDtypeStruct(level_table.shape, f32))
    hbm = pl.BlockSpec(memory_space=pltpu.HBM)
    body = functools.partial(kernel, span, wide, length * span, levels, heads, length)
    strip = (heads, length, DH)
    square = (levels, heads, DH, DH)
    parts = pl.pallas_call(
        body,
        out_shape=outs,
        in_specs=[any_spec] * 4 + [vmem, vmem, pl.BlockSpec(memory_space=pltpu.SMEM)],
        out_specs=(vmem, vmem, vmem, vmem),
        scratch_shapes=[
            pltpu.VMEM(strip, bf16), pltpu.VMEM(strip, bf16), pltpu.VMEM(strip, bf16), pltpu.VMEM(strip, bf16),
            pltpu.VMEM(strip, f32), pltpu.VMEM(strip, f32), pltpu.VMEM(strip, f32),
            pltpu.VMEM(square, f32), pltpu.VMEM(square, f32), pltpu.VMEM(square, f32), pltpu.VMEM(square, f32),
            pltpu.VMEM((heads, DH, DH), f32),
            pltpu.VMEM((heads, DH, levels * DH), bf16),
            pltpu.VMEM((heads, DH, DH), bf16),
            pltpu.VMEM((1, length), f32),
            pltpu.VMEM((levels, length, DH), f32),
            pltpu.VMEM((8, length), f32),
            pltpu.VMEM((levels, length, DH), f32),
            pltpu.VMEM((span,) + level_table.shape, f32),
            pltpu.VMEM((wide,) + level_table.shape, f32),
            pltpu.VMEM((level_table.shape[1], length), bf16),
            dma((4, heads)),
            pltpu.SemaphoreType.REGULAR((levels,)),
            dma((levels, CHUNKS)), dma((levels, CHUNKS)), dma((levels, CHUNKS)), dma((levels, CHUNKS)),
            dma((span,)), dma((span,)), dma((wide,)), dma((wide,)),
        ],
        compiler_params=pltpu.CompilerParams(
            collective_id=0, has_side_effects=True, vmem_limit_bytes=46 * 2 ** 20
        ),
        name="loglinear",
    )(queries, keys, values, out_grad, level_table, table_index.reshape(1, length), reach)
    return pl.pallas_call(
        finish,
        out_shape=outs,
        in_specs=[vmem] * 4,
        out_specs=(hbm, hbm, hbm, hbm),
        scratch_shapes=[dma((3 * PIECES + 1,))],
        compiler_params=pltpu.CompilerParams(vmem_limit_bytes=2 ** 20),
        name="finish",
    )(*parts)


def solution(mesh):
    return jax.shard_map(
        local,
        mesh=mesh,
        in_specs=(
            P("seq", "head"),
            P("seq", "head"),
            P("seq", "head"),
            P("seq", "head"),
            P(),
            P("seq"),
            P("seq"),
        ),
        out_specs=(P("seq", "head"), P("seq", "head"), P("seq", "head"), P()),
        check_vma=False,
    )
```
